32 devices in a mesh: dp: 8 (over z, y), grp: 4 (over x, core).
Axes of the slice: x: 2, y: 2, z: 4, core: 2. Of those that a mesh axis runs over, the one named last changes fastest.
Arguments:
- activations: bfloat16 [32, 512, 768], P('dp', None, 'grp'), may hold values from -6 to 6, as said below
- cotangent: bfloat16 [32, 512, 768], P('dp', None, 'grp'), may hold values from -6 to 6
- lengths: int32 [32], P('dp'), may hold values from 64 to 512
- triple_weight: bfloat16 [2, 4, 192, 576], P(None, 'grp'), may hold values from -0.25980762 to 0.25980762, as said below
- triple_bias: float32 [2, 2, 768], P(None, None, 'grp'), may hold values from -1.8 to 1.8, as said below
- output_weight: bfloat16 [2, 768, 768], replicated, may hold values from -1.75 to 1.75
- output_bias: float32 [2, 768], replicated, may hold values from -1.75 to 1.75
- first_gain: float32 [2, 768], replicated, may hold values from 0.25 to 1.75
- first_shift: float32 [2, 768], replicated, may hold values from -1.75 to 1.75
- widen_weight: bfloat16 [2, 4, 192, 768], P(None, 'grp'), may hold values from -0.4375 to 0.4375
- widen_bias: float32 [2, 3072], P(None, 'grp'), may hold values from -1.75 to 1.75
- shrink_weight: bfloat16 [2, 4, 768, 192], P(None, 'grp'), may hold values from -0.21875 to 0.21875
- narrow_bias: float32 [2, 768], P(None, 'grp'), may hold values from -1.75 to 1.75
- second_gain: float32 [2, 768], P(None, 'grp'), may hold values from 0.25 to 1.75
- second_shift: float32 [2, 768], P(None, 'grp'), may hold values from -1.75 to 1.75
Outputs:
- layer_output: bfloat16 [32, 512, 768], P('dp', None, 'grp')
- input_gradient: float32 [32, 512, 768], P('dp', None, 'grp')
- triple_weight_gradient: float32 [2, 4, 192, 576], P(None, 'grp')
- triple_bias_gradient: float32 [2, 2, 768], P(None, None, 'grp')
- output_weight_gradient: float32 [2, 768, 768], replicated
- output_bias_gradient: float32 [2, 768], replicated
- first_gain_gradient: float32 [2, 768], replicated
- first_shift_gradient: float32 [2, 768], replicated
- widen_weight_gradient: float32 [2, 4, 192, 768], P(None, 'grp')
- widen_bias_gradient: float32 [2, 3072], P(None, 'grp')
- narrow_weight_gradient: float32 [2, 4, 768, 192], P(None, 'grp')
- narrow_bias_gradient: float32 [2, 768], P(None, 'grp')
- second_norm_gain_gradient: float32 [2, 768], P(None, 'grp')
- second_shift_gradient: float32 [2, 768], P(None, 'grp')
The draws below stay inside these ranges and needn't reach their ends.
Inputs may be any that keep to these rules, and one draw needn't show every extreme that they name: `activations`: independent entries of order one. `triple_weight`: independent entries with deviation about 192 ** -0.5. `triple_bias`: independent entries with deviation about 0.3.
All inputs are finite; a program needn't handle non-finite values.
Results may differ from the reference program's by a relative error of at most 0.015.
Values may be sent and summed in bfloat16 or wider, within the bound.
A program may use at most 192 MiB of HBM per device.

```python
import jax
import jax.numpy as jnp
from jax import lax

D = 768
HEADS = 12
HEAD = 64
FF = 3072
GROUPS = 4
LAYERS = 2
SEQ_LEN = 512
GC = 192
FC = 768
SEQS = 32


def drawn_entries(key, shape, deviation):
    return jnp.clip(jax.random.normal(key, shape, jnp.float32), -3.5, 3.5) * deviation


def draw_activations(key, part):
    return drawn_entries(jax.random.fold_in(key, 11), (SEQS, SEQ_LEN, D), 1.0).astype(jnp.bfloat16)


def draw_triple_weight(key, part):
    return drawn_entries(jax.random.fold_in(key, 12), (LAYERS, GROUPS, GC, 3 * GC), GC ** (-0.5)).astype(jnp.bfloat16)


def draw_triple_bias(key, part):
    return drawn_entries(jax.random.fold_in(key, 13), (LAYERS, 2, D), 0.3)


def place_ends(values, key, smallest, top_value):
    spot = [jax.random.randint(jax.random.fold_in(key, axis), (), 0, length) for axis, length in enumerate(values.shape)]
    main_axis = values.shape.index(max(values.shape))
    next_to = spot[:main_axis] + [(spot[main_axis] + 1) % values.shape[main_axis]] + spot[main_axis + 1:]
    return values.at[tuple(spot)].set(smallest).at[tuple(next_to)].set(top_value)


def shard_levels(rng, extent, split, smallest, top_value):
    level = 1.0
    for position, shards_of in split:
        draws = jax.random.uniform(jax.random.fold_in(jax.random.fold_in(rng, 6), position), (shards_of,), jnp.float32, smallest / len(split), top_value / len(split))
        level = level * jnp.repeat(jnp.exp(draws), extent[position] // shards_of).reshape((-1,) + (1,) * (len(extent) - 1 - position))
    return level


def bell_draw(own_key, dims, width, bound, shards=(), kind=jnp.bfloat16):
    level = shard_levels(own_key, dims, shards, -0.22, 0.18) if shards else 1.0
    drawn = jax.random.normal(own_key, dims, jnp.float32) * width * level
    return jnp.minimum(jnp.maximum(drawn, -bound), bound).astype(kind)


def setup_inputs(seed: int = 0) -> dict:
    key_of = jax.random.split(jax.random.key(seed), 16)
    return {
        "activations": draw_activations(jax.random.fold_in(key_of[15], 71), 0),
        "cotangent": bell_draw(key_of[1], (SEQS, SEQ_LEN, D), 1.0, 6.0, ((0, 8), (2, 4))),
        "lengths": place_ends(jax.random.randint(key_of[2], (SEQS,), SEQ_LEN // 8, SEQ_LEN + 1), jax.random.fold_in(key_of[2], 1), SEQ_LEN // 8, SEQ_LEN).astype(jnp.int32),
        "triple_weight": draw_triple_weight(jax.random.fold_in(key_of[15], 71), 0),
        "triple_bias": draw_triple_bias(jax.random.fold_in(key_of[15], 71), 0),
        "output_weight": bell_draw(key_of[5], (LAYERS, D, D), (D // 64) ** -0.5, 1.75),
        "output_bias": bell_draw(key_of[6], (LAYERS, D), 0.3, 1.75, (), jnp.float32),
        "first_gain": jnp.clip(1.0 + 0.15 * jax.random.normal(key_of[7], (LAYERS, D), jnp.float32), 0.25, 1.75),
        "first_shift": bell_draw(key_of[8], (LAYERS, D), 0.3, 1.75, (), jnp.float32),
        "widen_weight": bell_draw(key_of[9], (LAYERS, GROUPS, GC, FC), GC ** -0.5, 0.4375, ((1, 4),)),
        "widen_bias": bell_draw(key_of[10], (LAYERS, FF), 0.3, 1.75, ((1, 4),), jnp.float32),
        "shrink_weight": bell_draw(key_of[11], (LAYERS, GROUPS, FC, GC), FC ** -0.5, 0.21875, ((1, 4),)),
        "narrow_bias": bell_draw(key_of[12], (LAYERS, D), 0.3, 1.75, ((1, 4),), jnp.float32),
        "second_gain": jnp.clip(1.0 + 0.15 * jax.random.normal(key_of[13], (LAYERS, D), jnp.float32), 0.25, 1.75),
        "second_shift": bell_draw(key_of[14], (LAYERS, D), 0.3, 1.75, ((1, 4),), jnp.float32),
    }


@jax.custom_vjp
def low(v):
    return lax.optimization_barrier(v.astype(jnp.bfloat16)).astype(jnp.float32)

@jax.custom_vjp
def low_back(v):
    return v

def low_keep(v):
    return (low(v), None)

def low_pass(kept, grad):
    return (grad,)

def back_keep(v):
    return (v, None)

def back_low(kept, grad):
    return (low(grad),)
low.defvjp(low_keep, low_pass)
low_back.defvjp(back_keep, back_low)
EPSILON = 1e-05
FULL_PRECISION = lax.Precision.HIGHEST

def normalize(rows, gain, shift):
    center = rows - lax.optimization_barrier(jnp.mean(rows, axis=-1, keepdims=True))
    inverse = lax.rsqrt(lax.optimization_barrier(jnp.mean(center * center, axis=-1, keepdims=True)) + EPSILON)
    return center * inverse * gain + shift

def attend_one(inputs):
    queries, keys, values, length = inputs
    query_heads = queries.reshape(SEQ_LEN, HEADS, HEAD)
    key_heads = keys.reshape(SEQ_LEN, HEADS, HEAD)
    value_heads = values.reshape(SEQ_LEN, HEADS, HEAD)
    scores = jnp.einsum('qhd,khd->hqk', query_heads, key_heads, precision=FULL_PRECISION) * HEAD ** (-0.5)
    scores = low_back(scores)
    visible = jnp.arange(SEQ_LEN).astype(jnp.int32) < length
    scores = jnp.where(visible[None, None, :], scores, -1e+30)
    expon = jnp.exp(scores - lax.optimization_barrier(jnp.max(scores, axis=-1, keepdims=True)))
    probs = expon / lax.optimization_barrier(jnp.sum(expon, axis=-1, keepdims=True))
    mixed = jnp.einsum('hqk,khd->qhd', low(probs), value_heads, precision=FULL_PRECISION)
    return mixed.reshape(SEQ_LEN, D)

def one_layer(inputs, lengths, weights, layer_params):
    triple_weight, triple_bias, output_weight, output_bias, first_gain, first_shift, widen_weight, widen_bias, shrink_weight, narrow_bias, second_gain, second_shift = weights
    rounded = low(inputs)
    grouped = rounded.reshape(SEQS, SEQ_LEN, GROUPS, GC)
    projected = jnp.einsum('slgc,gce->slge', grouped, triple_weight[layer_params], precision=FULL_PRECISION)
    queries = low_back(low(projected[..., :GC] + triple_bias[layer_params, 0].reshape(GROUPS, GC)))
    keys = low_back(low(projected[..., GC:2 * GC]))
    values = low_back(low(projected[..., 2 * GC:] + triple_bias[layer_params, 1].reshape(GROUPS, GC)))
    shape = (SEQS, SEQ_LEN, D)
    attended = lax.map(jax.checkpoint(attend_one), (queries.reshape(shape), keys.reshape(shape), values.reshape(shape), lengths))
    attended = low_back(low(attended)).reshape(-1, D)
    branch = low_back(jnp.dot(attended, output_weight[layer_params], precision=FULL_PRECISION) + output_bias[layer_params])
    before = low_back(rounded).reshape(-1, D) + branch
    hidden = low_back(low(normalize(before, first_gain[layer_params], first_shift[layer_params])))
    grouped_hidden = hidden.reshape(-1, GROUPS, GC)
    widened = jnp.einsum('rgc,gcf->rgf', grouped_hidden, widen_weight[layer_params], precision=FULL_PRECISION)
    widened = low_back(widened + widen_bias[layer_params].reshape(GROUPS, FC))
    gelu_output = low(jax.nn.gelu(widened, approximate=False))
    shrunk_hidden = jnp.einsum('jsl,sli->jsi', gelu_output, shrink_weight[layer_params], precision=FULL_PRECISION)
    shrunk_hidden = low_back(shrunk_hidden + narrow_bias[layer_params].reshape(GROUPS, GC))
    after = (grouped_hidden + shrunk_hidden).reshape(-1, D)
    return normalize(after, second_gain[layer_params], second_shift[layer_params]).reshape(shape)

def reference(activations, cotangent, lengths, triple_weight, triple_bias, output_weight, output_bias, first_gain, first_shift, widen_weight, widen_bias, shrink_weight, narrow_bias, second_gain, second_shift):
    floats = tuple((array.astype(jnp.float32) for array in (activations, triple_weight, triple_bias, output_weight, output_bias, first_gain, first_shift, widen_weight, widen_bias, shrink_weight, narrow_bias, second_gain, second_shift)))

    def forward(inputs, *weights):
        current = inputs
        for layer_params in range(LAYERS):
            current = one_layer(current, lengths, weights, layer_params)
        return current
    output, pullback = jax.vjp(forward, *floats)
    grads = pullback(cotangent.astype(jnp.float32))
    return (output.astype(jnp.bfloat16), grads[0], grads[1], grads[2], grads[3], grads[4], grads[5], grads[6], grads[7], grads[8], grads[9], grads[10], grads[11], grads[12])
```

```python
import functools
import math

import jax
import jax.numpy as jnp
from jax import lax
from jax.experimental import pallas as pl
from jax.experimental.pallas import tpu as pltpu
from jax.sharding import PartitionSpec as P

HEAD = 64
EPSILON = 1e-05
MASKED = -1e30
F32 = jnp.float32
BF16 = jnp.bfloat16
MESH = pl.DeviceIdType.MESH
NN = (((1,), (0,)), ((), ()))
NT = (((1,), (1,)), ((), ()))
ONES = 16


def mm(left, right, dims=NN):
    return lax.dot_general(left, right, dims, preferred_element_type=F32)


def lanes(block):
    total = block[:, 0:128]
    for start in range(128, block.shape[1], 128):
        total = total + block[:, start : start + 128]
    return total


def pack(first, second):
    pieces = []
    for row in (first, second):
        pieces += [row[:, start : start + 128] for start in range(0, row.shape[1], 128)]
    return jnp.concatenate(pieces, axis=0)


def unpack(tile):
    return jnp.concatenate([tile[k : k + 1] for k in range(tile.shape[0])], axis=1)


def phi_of(u):
    return 0.5 * (1.0 + lax.erf(u * (1.0 / math.sqrt(2.0))))


def body(
    depth,
    seqs,
    ndp,
    ngrp,
    tokens,
    gc,
    fc,
    part_rows,
    lens,
    x_hbm,
    ct,
    tw,
    tb,
    wo_hbm,
    bo,
    fg,
    fs,
    ww,
    bw,
    ws,
    nb,
    sg,
    ss,
    ytok,
    gx_hbm,
    grads_hbm,
    wog_hbm,
    vec_hbm,
    xT,
    qkT,
    vtok,
    eT,
    rls,
    og,
    oown,
    xh1,
    inv1,
    hT,
    xh2,
    inv2,
    twT,
    wkp,
    wvp,
    vrow,
    wwT,
    wsT,
    woT,
    wog,
    cola,
    colb,
    rowa,
    qz,
    kmb,
    vaug,
    goz,
    abuf,
    gub,
    ghs,
    gqkv,
    r1s,
    r2s,
    gy,
    gxs,
    accw,
    accs,
    acco,
    acct,
    accv,
    vec8,
    gbuf,
    rsbuf,
    stat_out,
    stat_in,
    local_sem,
    gx_sem,
    send_own,
    send_pair,
    send_relay,
    recv_far,
    recv_pair,
    recv_relay,
    stat_send,
    stat_recv,
    rs_send,
    rs_recv,
    ag_send,
    ag_recv,
    ag_own,
    fin_own,
    fin_send,
    fin_recv,
):
    heads = gc // HEAD
    items = depth * seqs
    width = gc * ngrp
    chunk = part_rows // ndp
    half = tokens // 128
    dp = lax.axis_index("dp")
    g = lax.axis_index("grp")
    pair, far = g ^ 1, g ^ 2
    near_far = g ^ 3

    barrier = pltpu.get_barrier_semaphore()

    def greet(k, carry):
        pl.semaphore_signal(barrier, inc=1, device_id=(lax.rem(dp + k, ndp), g), device_id_type=MESH)
        return carry

    lax.fori_loop(1, ndp, greet, 0)
    for other in (pair, far, near_far):
        pl.semaphore_signal(barrier, inc=1, device_id=(dp, other), device_id_type=MESH)

    wo_copies = []
    for l in range(depth):
        for part in range(2):
            wo_copies.append(
                pltpu.make_async_copy(
                    wo_hbm.at[l, pl.ds(part * (width // 2), width // 2), :],
                    gbuf.at[2 * l + part, pl.ds(0, width // 2), :],
                    local_sem.at[2 * l + part],
                )
            )
            wo_copies[-1].start()
    x_copy = pltpu.make_async_copy(x_hbm, ytok, local_sem.at[2 * depth])
    x_copy.start()
    own_copies = []
    for l in range(depth):
        own_copies.append(
            pltpu.make_async_copy(
                wo_hbm.at[l, pl.ds(pl.multiple_of(g * gc, 64), gc), :],
                wog.at[l],
                local_sem.at[2 * depth + 1 + l],
            )
        )
        own_copies[-1].start()

    lane = lax.broadcasted_iota(jnp.int32, (1, 128), 1)
    for l in range(depth):
        twT[l] = tw[l].T
        wwT[l] = ww[l].T
        wsT[l] = ws[l].T
        wkp[l] = jnp.zeros(wkp.shape[1:], BF16)
        wvp[l] = jnp.zeros(wvp.shape[1:], BF16)
        vrow[l] = jnp.zeros(vrow.shape[1:], F32)
        for h in range(heads):
            wkp[l, :, h * 128 : h * 128 + HEAD] = tw[l, :, gc + h * HEAD : gc + (h + 1) * HEAD]
            wvp[l, :, h * 128 : h * 128 + HEAD] = tw[
                l, :, 2 * gc + h * HEAD : 2 * gc + (h + 1) * HEAD
            ]
            vrow[l, 0:1, h * 128 : (h + 1) * 128] = jnp.where(
                (lane == HEAD) | (lane == HEAD + 1), 1.0, 0.0
            )
            vrow[l, 0:1, h * 128 : h * 128 + HEAD] = tb[l, 1:2, h * HEAD : (h + 1) * HEAD]
        rowa[...] = jnp.zeros(rowa.shape, F32)
        rowa[0:1] = bo[l : l + 1]
        rowa[1:2] = fg[l : l + 1]
        rowa[2:3] = fs[l : l + 1]
        rowa[3:4] = bw[l : l + 1]
        cola[l] = rowa[...].T
        rowa[0:2, 0:gc] = tb[l]
        rowa[2:3, 0:gc] = nb[l : l + 1]
        rowa[3:4, 0:gc] = sg[l : l + 1]
        rowa[4:5, 0:gc] = ss[l : l + 1]
        colb[l] = rowa[:, 0:gc].T
    ones_rows = jnp.ones((ONES, tokens), BF16)
    for i in range(items):
        xT[i, gc : gc + ONES] = ones_rows
        hT[i, gc : gc + ONES] = ones_rows
        oown[i, gc : gc + ONES] = ones_rows
    row = lax.broadcasted_iota(jnp.int32, (HEAD, tokens), 0)
    for h in range(heads):
        qz[h, HEAD : 2 * HEAD] = jnp.where(row == 0, 1.0, 0.0).astype(BF16)
        goz[h, HEAD : 2 * HEAD] = jnp.zeros((HEAD, tokens), BF16)
        vaug[h, HEAD : HEAD + ONES] = ones_rows
    x_copy.wait()
    for s in range(seqs):
        xT[s, 0:gc] = ytok[s].T
    for copy in wo_copies:
        copy.wait()
    for copy in own_copies:
        copy.wait()
    for l in range(depth):
        for j in range(ngrp):

            @pl.when(g == j)
            def _(l=l, j=j):
                for part in range(2):
                    woT[l, :, part * (width // 2) : (part + 1) * (width // 2)] = gbuf[
                        2 * l + part, 0 : width // 2, j * gc : (j + 1) * gc
                    ].T

    pl.semaphore_wait(barrier, ndp - 1 + 3)

    def block_of(i, owner):
        return og.at[i, pl.ds(pl.multiple_of(owner * gc, 64), gc), :]

    def to_pair(i, p):
        return pltpu.make_async_remote_copy(
            block_of(i, g), block_of(i, g), send_pair.at[p, i], recv_pair.at[p, i], (dp, pair), device_id_type=MESH
        )

    def to_far(i, p):
        return pltpu.make_async_remote_copy(
            block_of(i, g), block_of(i, g), send_own.at[p, i], recv_far.at[p, i], (dp, far), device_id_type=MESH
        )

    def relay(i, p):
        return pltpu.make_async_remote_copy(
            block_of(i, far), block_of(i, far), send_relay.at[p, i], recv_relay.at[p, i], (dp, pair), device_id_type=MESH
        )

    def send_block(i, p):
        to_far(i, p).start()
        to_pair(i, p).start()

    def relay_block(i, p):
        to_far(i, p).wait_recv()
        relay(i, p).start()

    def finish_block(i, p):
        to_pair(i, p).wait()
        relay(i, p).wait()
        to_far(i, p).wait_send()

    def stat_copy(kind, i, k):
        other = g ^ (k + 1)
        return pltpu.make_async_remote_copy(
            stat_out.at[kind, i],
            stat_in.at[kind, i, k],
            stat_send.at[kind, i],
            stat_recv.at[kind, i],
            (dp, other),
            device_id_type=MESH,
        )

    def send_stats(kind, i, first, second):
        stat_out[kind, i] = pack(first, second)
        for k in range(ngrp - 1):
            stat_copy(kind, i, k).start()

    def wait_stats(kind, i):
        every = stat_in.at[kind, i]
        pltpu.make_async_copy(every, every, stat_recv.at[kind, i]).wait()
        pltpu.make_async_copy(every, every, stat_send.at[kind, i]).wait()
        return [stat_out[kind, i]] + [stat_in[kind, i, k] for k in range(ngrp - 1)]

    def moments(tiles):
        mean = (tiles[0][:half] + tiles[1][:half] + tiles[2][:half] + tiles[3][:half]) * (1.0 / ngrp)
        second = tiles[0][half:] + tiles[1][half:] + tiles[2][half:] + tiles[3][half:]
        for tile in tiles:
            off = tile[:half] - mean
            second = second + gc * (off * off)
        inverse = lax.rsqrt(second * (1.0 / width) + EPSILON)
        return unpack(mean), unpack(inverse)

    def two_means(tiles):
        total = (tiles[0] + tiles[1] + tiles[2] + tiles[3]) * (1.0 / width)
        return unpack(total[:half]), unpack(total[half:])

    def local_moments(rows):
        mean = jnp.sum(rows, axis=0, keepdims=True) * (1.0 / gc)
        off = rows - mean
        return mean, jnp.sum(off * off, axis=0, keepdims=True)

    def own(l, k):
        return cola[l, pl.ds(pl.multiple_of(g * gc, 64), gc), k : k + 1]

    def attend(i):
        l = i // seqs
        s = i - l * seqs
        length = lens[s]
        xt = xT[i, 0:gc]
        qf = mm(twT[l, 0:gc], xt) + colb[l, :, 0:1]
        q = qf.astype(BF16) * jnp.asarray(HEAD ** (-0.5), BF16)
        qkT[i, 0:gc] = q
        for h in range(heads):
            qz[h, 0:HEAD] = q[h * HEAD : (h + 1) * HEAD]
        qkT[i, gc : 2 * gc] = mm(twT[l, gc : 2 * gc], xt).astype(BF16)
        v = (mm(twT[l, 2 * gc : 3 * gc], xt) + colb[l, :, 1:2]).astype(BF16)
        for h in range(heads):
            vaug[h, 0:HEAD] = v[h * HEAD : (h + 1) * HEAD]
        xk = ytok[s]
        key = lax.broadcasted_iota(jnp.int32, (tokens, 128), 0)
        spot = lax.broadcasted_iota(jnp.int32, (tokens, 128), 1)
        hide = jnp.where((key >= length) & (spot == HEAD), MASKED, 0.0)
        for h in range(heads):
            cols = slice(h * 128, (h + 1) * 128)
            kmb[h] = (mm(xk, wkp[l, :, cols]) + hide).astype(BF16)
            vtok[i, h] = (mm(xk, wvp[l, :, cols]) + vrow[l, 0:1, cols]).astype(BF16)

        def head(h, carry):
            st = mm(kmb[h], qz[h])
            top = jnp.max(st, axis=0, keepdims=True)
            e = jnp.exp(st - top).astype(BF16)
            eT[i * heads + h] = e
            ot = mm(vaug[h], e)
            rl = 1.0 / ot[HEAD : HEAD + 1]
            rls[i * heads + h] = rl
            o = (ot[0:HEAD] * rl).astype(BF16)
            oown[i, pl.ds(pl.multiple_of(h * HEAD, 64), HEAD)] = o
            og[i, pl.ds(pl.multiple_of(g * gc + h * HEAD, 64), HEAD)] = o
            return carry

        lax.fori_loop(0, heads, head, 0)
        send_block(i, 0)

    def mix(i):
        l = i // seqs
        finish_block(i, 0)
        r1 = xT[i, 0:gc].astype(F32) + mm(woT[l], og[i]) + own(l, 0)
        r1s[...] = r1
        send_stats(0, i, *local_moments(r1))

    def feed(i):
        l = i // seqs
        mean, inverse = moments(wait_stats(0, i))
        xhat = (r1s[...] - mean) * inverse
        xh1[i] = xhat.astype(BF16)
        inv1[i] = inverse
        h = (xhat * own(l, 1) + own(l, 2)).astype(BF16)
        hT[i, 0:gc] = h
        for c in range(0, fc, 128):
            u = mm(wwT[l, c : c + 128], h) + cola[l, c : c + 128, 3:4]
            abuf[c : c + 128] = (u * phi_of(u)).astype(BF16)
        r2 = h.astype(F32) + mm(wsT[l], abuf[...]) + colb[l, :, 2:3]
        r2s[i % 2] = r2
        send_stats(1, i, *local_moments(r2))

    def close(i):
        l = i // seqs
        s = i - l * seqs
        mean, inverse = moments(wait_stats(1, i))
        xhat = (r2s[i % 2] - mean) * inverse
        xh2[i] = xhat.astype(BF16)
        inv2[i] = inverse
        y = (xhat * colb[l, :, 3:4] + colb[l, :, 4:5]).astype(BF16)
        ytok[s] = y.T

        @pl.when(l < depth - 1)
        def _():
            xT[jnp.minimum(i + seqs, items - 1), 0:gc] = y

    def place(j):
        l = depth - 1 - j // seqs
        s = j % seqs
        return l, s, l * seqs + s

    def back_open(j):
        l, s, i = place(j)

        @pl.when(l == depth - 1)
        def _():
            gy[s] = ct[s].T.astype(F32)

        @pl.when(s == 0)
        def _():
            for k in range(accv.shape[1]):
                accv[l, k] = jnp.zeros(accv.shape[2:], F32)

        grad = gy[s]
        xhat = xh2[i].astype(F32)
        t = grad * colb[l, :, 3:4]
        accv[l, 0] += lanes(grad * xhat)
        accv[l, 1] += lanes(grad)
        send_stats(
            2, i, jnp.sum(t, axis=0, keepdims=True), jnp.sum(t * xhat, axis=0, keepdims=True)
        )

    def back_feed(j):
        l, s, i = place(j)

        @pl.when(s == 0)
        def _():
            accw[...] = jnp.zeros(accw.shape, F32)
            accs[...] = jnp.zeros(accs.shape, F32)

        mean_t, mean_x = two_means(wait_stats(2, i))
        t = gy[s] * colb[l, :, 3:4]
        g2 = inv2[i] * (t - mean_t - xh2[i].astype(F32) * mean_x)
        gf = g2.astype(BF16)
        accv[l, 2] += lanes(gf.astype(F32))
        h = hT[i, 0:gc]
        for c in range(0, fc, 128):
            u = mm(wwT[l, c : c + 128], h) + cola[l, c : c + 128, 3:4]
            big = phi_of(u)
            abuf[c : c + 128] = (u * big).astype(BF16)
            slope = big + u * jnp.exp(-0.5 * u * u) * (1.0 / math.sqrt(2.0 * math.pi))
            gub[c : c + 128] = (mm(ws[l, c : c + 128], gf) * slope).astype(BF16)
        accs[...] += mm(gf, abuf[...], NT)
        accw[...] += mm(hT[i], gub[...], NT)
        gh = (g2 + mm(ww[l], gub[...])).astype(BF16)
        ghs[...] = gh
        ghf = gh.astype(F32)
        xhat = xh1[i].astype(F32)
        accv[l, 3] += lanes(ghf * xhat)
        accv[l, 4] += lanes(ghf)
        t1 = ghf * own(l, 1)
        send_stats(
            3, i, jnp.sum(t1, axis=0, keepdims=True), jnp.sum(t1 * xhat, axis=0, keepdims=True)
        )

    def back_norm(j):
        l, s, i = place(j)
        mean_t, mean_x = two_means(wait_stats(3, i))
        t1 = ghs[...].astype(F32) * own(l, 1)
        g1 = inv1[i] * (t1 - mean_t - xh1[i].astype(F32) * mean_x)
        og[i, pl.ds(pl.multiple_of(g * gc, 64), gc)] = g1.astype(BF16)
        send_block(i, 1)

    def gx_copy(s):
        return pltpu.make_async_copy(gxs.at[s % 2], gx_hbm.at[s], gx_sem.at[s % 2])

    def back_attend(j):
        l, s, i = place(j)
        finish_block(i, 1)

        @pl.when(s == 0)
        def _():
            acco[...] = jnp.zeros(acco.shape, F32)
            acct[...] = jnp.zeros(acct.shape, F32)

        acco[...] += mm(oown[i], og[i], NT)
        go = mm(wog[l], og[i]).astype(BF16)
        for h in range(heads):
            goz[h, 0:HEAD] = go[h * HEAD : (h + 1) * HEAD]
        edge = lax.broadcasted_iota(jnp.int32, (ONES, tokens), 0)

        def head(h, carry):
            base = pl.multiple_of(h * HEAD, 64)
            gos = (goz[h, 0:HEAD].astype(F32) * rls[i * heads + h]).astype(BF16)
            delta = jnp.sum(
                gos.astype(F32) * oown[i, pl.ds(base, HEAD)].astype(F32), axis=0, keepdims=True
            )
            high = delta.astype(BF16).astype(F32)
            goz[h, 0:HEAD] = gos
            goz[h, HEAD : HEAD + ONES] = jnp.where(
                edge == 0, -high, jnp.where(edge == 1, high - delta, 0.0)
            ).astype(BF16)
            e = eT[i * heads + h]
            gs = (e.astype(F32) * mm(vtok[i, h], goz[h])).astype(BF16)
            gqkv[pl.ds(base, HEAD)] = (
                mm(qkT[i, pl.ds(pl.multiple_of(gc + h * HEAD, 64), HEAD)], gs) * HEAD ** (-0.5)
            ).astype(BF16)
            gqkv[pl.ds(pl.multiple_of(gc + h * HEAD, 64), HEAD)] = mm(
                qkT[i, pl.ds(base, HEAD)], gs, NT
            ).astype(BF16)
            gqkv[pl.ds(pl.multiple_of(2 * gc + h * HEAD, 64), HEAD)] = mm(gos, e, NT).astype(BF16)
            return carry

        lax.fori_loop(0, heads, head, 0)
        acct[...] += mm(xT[i], gqkv[...], NT)
        gx = mm(tw[l], gqkv[...]) + og[i, pl.ds(pl.multiple_of(g * gc, 64), gc)].astype(F32)

        @pl.when(l > 0)
        def _():
            gy[s] = gx

        @pl.when(l == 0)
        def _():
            @pl.when(s >= 2)
            def _():
                gx_copy(s).wait()

            gxs[s % 2] = gx.T
            gx_copy(s).start()

    def pack_feed(l):
        gbuf[2 * l, 0:gc] = accw[0:gc].astype(BF16)
        gbuf[2 * l, gc : 2 * gc] = accs[...].astype(BF16)
        vec8[l, 0:1] = accw[gc : gc + 1]

    def pack_attend(l):
        q = 2 * l + 1
        gbuf[q, 0:gc] = acco[0:gc].astype(BF16)
        gbuf[q, gc : 2 * gc, 0 : 3 * gc] = acct[0:gc].astype(BF16)
        vec8[l, 1:2] = acco[gc : gc + 1]
        vec8[l, 2:8] = jnp.zeros((6, width), F32)
        vec8[l, 2:3, 0 : 3 * gc] = acct[gc : gc + 1]
        for k in range(accv.shape[1]):
            vec8[l, 3 + k : 4 + k, 0:gc] = jnp.sum(accv[l, k].T, axis=0, keepdims=True)
        vec = vec8[l]
        for k in range(0, width // 128, 2):
            both = jnp.concatenate(
                [vec[:, k * 128 : (k + 1) * 128], vec[:, (k + 1) * 128 : (k + 2) * 128]], axis=0
            )
            gbuf[q, gc + 8 * k : gc + 8 * k + 16, width - 128 : width] = both.astype(BF16)

    def rows_of(q, owner):
        return gbuf.at[q, pl.ds(pl.multiple_of(owner * chunk, 16), chunk), :]

    def summed_rows(q):
        return grads_hbm.at[q, pl.ds(pl.multiple_of(dp * chunk, 16), chunk), :]

    def scatter_copy(q, k):
        to = lax.rem(dp + k, ndp)
        return pltpu.make_async_remote_copy(
            rows_of(q, to), rsbuf.at[q % 2, k - 1], rs_send.at[q], rs_recv.at[q], (to, g), device_id_type=MESH
        )

    def gather_copy(q, k):
        to = lax.rem(dp + k, ndp)
        return pltpu.make_async_remote_copy(
            rows_of(q, dp), summed_rows(q), ag_send.at[q], ag_recv.at[q], (to, g), device_id_type=MESH
        )

    def own_rows(q):
        return pltpu.make_async_copy(rows_of(q, dp), summed_rows(q), ag_own.at[q])

    def start_all(copy, q):
        def step(k, carry):
            copy(q, k).start()
            return carry

        lax.fori_loop(1, ndp, step, 0)

    def wait_all(sem, q):
        every = rsbuf.at[q % 2]
        pltpu.make_async_copy(every, every, sem.at[q]).wait()

    def reduce_part(q):
        wait_all(rs_recv, q)
        wait_all(rs_send, q)
        mine = pl.ds(pl.multiple_of(dp * chunk, 16), chunk)

        def add(k, total):
            return total + rsbuf[q % 2, k].astype(F32)

        total = lax.fori_loop(0, ndp - 1, add, gbuf[q, mine].astype(F32))
        gbuf[q, mine] = total.astype(BF16)
        start_all(gather_copy, q)
        own_rows(q).start()

    def gathered_part(q):
        own_rows(q).wait()
        wait_all(ag_recv, q)
        wait_all(ag_send, q)

    def final_sources(l):
        q = 2 * l + 1
        return (
            grads_hbm.at[q, pl.ds(0, gc), :],
            grads_hbm.at[q, pl.ds(gc, 8 * (width // 128)), pl.ds(width - 128, 128)],
        )

    def final_own(l):
        targets = (wog_hbm.at[l, g], vec_hbm.at[l, g])
        return [
            pltpu.make_async_copy(source, target, fin_own.at[l, m])
            for m, (source, target) in enumerate(zip(final_sources(l), targets))
        ]

    def final_copies(l, owner, to, k):
        if k < 2:
            sources = final_sources(l)
        else:
            sources = (wog_hbm.at[l, owner], vec_hbm.at[l, owner])
        targets = (wog_hbm.at[l, owner], vec_hbm.at[l, owner])
        return [
            pltpu.make_async_remote_copy(
                sources[m], targets[m], fin_send.at[l, k, m], fin_recv.at[l, k, m], (dp, to), device_id_type=MESH
            )
            for m in range(2)
        ]

    def final_send(l):
        for copy in final_copies(l, g, far, 0) + final_copies(l, g, pair, 1) + final_own(l):
            copy.start()

    def final_relay(l):
        for copy in final_copies(l, g, far, 0):
            copy.wait_recv()
        for copy in final_copies(l, far, pair, 2):
            copy.start()

    def final_wait(l):
        for copy in final_own(l):
            copy.wait()
        for copy in final_copies(l, g, far, 0):
            copy.wait_send()
        for copy in final_copies(l, g, pair, 1) + final_copies(l, far, pair, 2):
            copy.wait()

    def within(value, limit, run):
        @pl.when((value >= 0) & (value < limit))
        def _():
            run(jnp.clip(value, 0, limit - 1))

    def at(now, when, run):
        @pl.when(now == when)
        def _():
            run()

    first = items

    def tick(t, carry):
        u = t - first
        within(t - 3, items, feed)
        within(t - 2, items, mix)
        within(t - 4, items, close)
        within(t, items, attend)
        within(u - 1, items, back_feed)
        within(u, items, back_open)
        within(u - 3, items, back_attend)
        within(u - 1, items, back_norm)
        within(t - 1, items, lambda i: relay_block(i, 0))
        within(u - 2, items, lambda j: relay_block(place(j)[2], 1))

        feed_done = u - seqs
        attend_done = u - seqs - 2

        @pl.when((feed_done >= 0) & (lax.rem(feed_done, seqs) == 0) & (feed_done < items))
        def _():
            l = depth - 1 - feed_done // seqs

            @pl.when(feed_done >= seqs)
            def _():
                gathered_part(jnp.minimum(2 * l + 2, 2 * depth - 2))

            pack_feed(l)
            start_all(scatter_copy, 2 * l)

        @pl.when((attend_done >= 0) & (lax.rem(attend_done, seqs) == 0) & (attend_done < items))
        def _():
            l = depth - 1 - attend_done // seqs
            pack_attend(l)
            start_all(scatter_copy, 2 * l + 1)
            reduce_part(2 * l)

        @pl.when((attend_done >= 2) & (lax.rem(attend_done, seqs) == 2) & (attend_done < items))
        def _():
            reduce_part(2 * (depth - 1 - attend_done // seqs) + 1)

        @pl.when((attend_done >= 3) & (lax.rem(attend_done, seqs) == 3) & (attend_done < items))
        def _():
            l = depth - 1 - attend_done // seqs
            gathered_part(2 * l + 1)
            final_send(l)

        return carry

    lax.fori_loop(0, first + items + 3, tick, 0)

    reduce_part(1)
    for l in range(depth - 1, 0, -1):
        final_relay(l)
    gathered_part(0)
    gathered_part(1)
    final_send(0)
    final_relay(0)
    for l in range(depth):
        final_wait(l)
    for s in range(seqs - 2, seqs):
        gx_copy(s).wait()


def shards(
    ndp,
    ngrp,
    activations,
    cotangent,
    lengths,
    triple_weight,
    triple_bias,
    output_weight,
    output_bias,
    first_gain,
    first_shift,
    widen_weight,
    widen_bias,
    shrink_weight,
    narrow_bias,
    second_gain,
    second_shift,
):
    seqs, tokens, gc = activations.shape
    depth = triple_weight.shape[0]
    fc = widen_weight.shape[-1]
    width = gc * ngrp
    heads = gc // HEAD
    items = depth * seqs
    parts = 2 * depth
    assert ngrp == 4 and seqs == 4 and depth == 2 and fc == width and 2 * tokens == 8 * 128
    part_rows = -(-2 * gc // (16 * ndp)) * 16 * ndp
    chunk = part_rows // ndp
    vec_rows = 8 * (width // 128)
    vmem = pl.BlockSpec(memory_space=pltpu.VMEM)
    hbm = pl.BlockSpec(memory_space=pl.ANY)
    smem = pl.BlockSpec(memory_space=pltpu.SMEM)
    dma = pltpu.SemaphoreType.DMA
    V = pltpu.VMEM
    scratch = [
        V((items, gc + ONES, tokens), BF16),
        V((items, 2 * gc, tokens), BF16),
        V((items, heads, tokens, 128), BF16),
        V((items * heads, tokens, tokens), BF16),
        V((items * heads, 1, tokens), F32),
        V((items, width, tokens), BF16),
        V((items, gc + ONES, tokens), BF16),
        V((items, gc, tokens), BF16),
        V((items, 1, tokens), F32),
        V((items, gc + ONES, tokens), BF16),
        V((items, gc, tokens), BF16),
        V((items, 1, tokens), F32),
        V((depth, 3 * gc, gc), BF16),
        V((depth, gc, heads * 128), BF16),
        V((depth, gc, heads * 128), BF16),
        V((depth, 8, heads * 128), F32),
        V((depth, fc, gc), BF16),
        V((depth, gc, fc), BF16),
        V((depth, gc, width), BF16),
        V((depth, gc, width), BF16),
        V((depth, width, 128), F32),
        V((depth, gc, 128), F32),
        V((128, width), F32),
        V((heads, 2 * HEAD, tokens), BF16),
        V((heads, tokens, 128), BF16),
        V((heads, HEAD + ONES, tokens), BF16),
        V((heads, 2 * HEAD, tokens), BF16),
        V((fc, tokens), BF16),
        V((fc, tokens), BF16),
        V((gc, tokens), BF16),
        V((3 * gc, tokens), BF16),
        V((gc, tokens), F32),
        V((2, gc, tokens), F32),
        V((seqs, gc, tokens), F32),
        V((2, tokens, gc), F32),
        V((gc + ONES, fc), F32),
        V((gc, fc), F32),
        V((gc + ONES, width), F32),
        V((gc + ONES, 3 * gc), F32),
        V((depth, 5, gc, 128), F32),
        V((depth, 8, width), F32),
        V((parts, part_rows, width), BF16),
        V((2, ndp - 1, chunk, width), BF16),
        V((4, items, 8, 128), F32),
        V((4, items, ngrp - 1, 8, 128), F32),
        dma((3 * depth + 1,)),
        dma((2,)),
        dma((2, items)),
        dma((2, items)),
        dma((2, items)),
        dma((2, items)),
        dma((2, items)),
        dma((2, items)),
        dma((4, items)),
        dma((4, items)),
        dma((parts,)),
        dma((parts,)),
        dma((parts,)),
        dma((parts,)),
        dma((parts,)),
        dma((depth, 2)),
        dma((depth, 3, 2)),
        dma((depth, 3, 2)),
    ]
    y, gx, grads, wog, vec = pl.pallas_call(
        functools.partial(body, depth, seqs, ndp, ngrp, tokens, gc, fc, part_rows),
        out_shape=(
            jax.ShapeDtypeStruct((seqs, tokens, gc), BF16),
            jax.ShapeDtypeStruct((seqs, tokens, gc), F32),
            jax.ShapeDtypeStruct((parts, part_rows, width), BF16),
            jax.ShapeDtypeStruct((depth, ngrp, gc, width), BF16),
            jax.ShapeDtypeStruct((depth, ngrp, vec_rows, 128), BF16),
        ),
        in_specs=[smem, hbm, vmem, vmem, vmem, hbm] + [vmem] * 9,
        out_specs=(vmem, hbm, hbm, hbm, hbm),
        scratch_shapes=scratch,
        compiler_params=pltpu.CompilerParams(
            collective_id=0, has_side_effects=True, vmem_limit_bytes=63 << 20
        ),
        name="layers",
    )(
        lengths,
        activations,
        cotangent,
        triple_weight.reshape(depth, gc, 3 * gc),
        triple_bias,
        output_weight,
        output_bias,
        first_gain,
        first_shift,
        widen_weight.reshape(depth, gc, fc),
        widen_bias,
        shrink_weight.reshape(depth, fc, gc),
        narrow_bias,
        second_gain,
        second_shift,
    )
    feed = grads[0::2]
    rest = grads[1::2]
    vec = vec.reshape(depth, ngrp, width // 128, 8, 128).transpose(0, 1, 3, 2, 4)
    vec = vec.reshape(depth, ngrp, 8, width).astype(F32)
    mine = lax.dynamic_index_in_dim(vec, lax.axis_index("grp"), 1, keepdims=False)
    shared = vec[:, :, :, :gc]
    return (
        y,
        gx,
        rest[:, gc : 2 * gc, : 3 * gc].astype(F32)[:, None],
        jnp.stack([mine[:, 2, :gc], mine[:, 2, 2 * gc : 3 * gc]], axis=1),
        wog.reshape(depth, width, width).astype(F32),
        mine[:, 1],
        shared[:, :, 6].reshape(depth, width),
        shared[:, :, 7].reshape(depth, width),
        feed[:, :gc].astype(F32)[:, None],
        mine[:, 0],
        feed[:, gc : 2 * gc].astype(F32).transpose(0, 2, 1)[:, None],
        mine[:, 5, :gc],
        mine[:, 3, :gc],
        mine[:, 4, :gc],
    )


def solution(mesh):
    ndp, ngrp = mesh.shape["dp"], mesh.shape["grp"]
    in_specs = (
        P("dp", None, "grp"),
        P("dp", None, "grp"),
        P("dp"),
        P(None, "grp", None, None),
        P(None, None, "grp"),
        P(),
        P(),
        P(),
        P(),
        P(None, "grp", None, None),
        P(None, "grp"),
        P(None, "grp", None, None),
        P(None, "grp"),
        P(None, "grp"),
        P(None, "grp"),
    )
    out_specs = (
        P("dp", None, "grp"),
        P("dp", None, "grp"),
        P(None, "grp", None, None),
        P(None, None, "grp"),
        P(),
        P(),
        P(),
        P(),
        P(None, "grp", None, None),
        P(None, "grp"),
        P(None, "grp", None, None),
        P(None, "grp"),
        P(None, "grp"),
        P(None, "grp"),
    )
    return jax.shard_map(
        functools.partial(shards, ndp, ngrp),
        mesh=mesh,
        in_specs=in_specs,
        out_specs=out_specs,
        check_vma=False,
    )
```
